128 devices in a mesh: dp: 2 (over core), segment: 4 (over x), rows: 16 (over z, y).
Axes of the slice: x: 4, y: 4, z: 4, core: 2. Of those that a mesh axis runs over, the one named last changes fastest.
Arguments:
- images: bfloat16 [8, 32, 32, 1024], P('dp', 'rows'), may hold values from -6 to 6
- cotangent: bfloat16 [8, 32, 32, 1024], P('dp', 'rows')
- pointwise: bfloat16 [8, 1024, 1024], P('segment'), may hold values from -0.1875 to 0.1875
- depthwise: float32 [8, 9, 1024], P('segment'), may hold values from -2 to 2
- norm_gain: float32 [8, 1024], P('segment'), may hold values from 0.25 to 1.75
- norm_shift: float32 [8, 1024], P('segment'), may hold values from -1.75 to 1.75
- cell_counts: int32 [4], P('segment'), may hold values from 1 to 2, as said below
- dilations: int32 [8], P('segment'), may hold values from 1 to 2, as said below
Outputs:
- section_outputs: bfloat16 [4, 8, 32, 32, 1024], P('segment', 'dp', 'rows')
- grad_pointwise: float32 [8, 1024, 1024], P('segment', ('dp', 'rows'))
- grad_depthwise: float32 [8, 9, 1024], P('segment', None, ('dp', 'rows'))
- grad_norm: float32 [8, 2, 1024], P('segment', None, ('dp', 'rows'))
The draws below stay inside these ranges and needn't reach their ends.
Inputs may be any that keep to these rules, and one draw needn't show every extreme that they name: `cell_counts`: some section has 2 active blocks and some section one. `dilations`: slot 0 of some section has rate 2.
All inputs are finite; a program needn't handle non-finite values.
Results may differ from the reference program's by a relative error of at most 0.014.
Values may be sent and summed in bfloat16 or wider, within the bound.
A program may use at most 64 MiB of HBM per device.

```python
import jax
import jax.numpy as jnp
from jax import lax

CHANS = 1024
DMAX = 2
CMAX = 2
MICRO = 2
IMG = 2
ROWS_DEV = 2
COLS = 32
SEGMENTS = 4
SLOTS = 8
HEIGHT = 32
BATCH = 8
N_DP = 2
N_ROWS = 16


def draw_cell_counts(key, part):
    counts = jax.random.randint(key, (SEGMENTS,), 1, CMAX + 1)
    order = jax.random.permutation(jax.random.fold_in(key, 7), SEGMENTS)
    counts = counts.at[order[0]].set(CMAX).at[order[1]].set(1)
    return counts.astype(jnp.int32)


def draw_dilations(key, part):
    rates = jax.random.randint(key, (SLOTS,), 1, DMAX + 1)
    order = jax.random.permutation(jax.random.fold_in(key, 11), SEGMENTS)
    rates = rates.at[order[0] * CMAX].set(DMAX).at[order[1] * CMAX].set(1)
    return rates.astype(jnp.int32)


def draw_cotangent(key, part):
    noise_key = jax.random.fold_in(key, 21)
    common_key = jax.random.fold_in(key, 22)
    shape = (BATCH, HEIGHT, COLS, CHANS)
    height_pos = jnp.arange(HEIGHT, dtype=jnp.float32) / max(HEIGHT - 1, 1)
    noise = jax.random.truncated_normal(noise_key, -6.0, 6.0, shape, jnp.float32)
    common = jax.random.normal(common_key, (CHANS,), jnp.float32)
    ramp = jnp.power(10.0, height_pos - 1.0)
    field = (noise + common[None, None, None, :]) * ramp[None, :, None, None]
    scale = 2.0 * (BATCH * HEIGHT * COLS) ** (-0.5)
    return (field * scale).astype(jnp.bfloat16)


def levels(stream_key, dims, split, low, top_value):
    loudness, own = 1.0, jax.random.fold_in(stream_key, 6)
    for dim, parts in split:
        steps = jnp.exp(jax.random.uniform(jax.random.fold_in(own, dim), (parts,), jnp.float32, low / len(split), top_value / len(split)))
        loudness = loudness * jnp.repeat(steps, dims[dim] // parts).reshape([-1 if axis == dim else 1 for axis in range(len(dims))])
    return loudness


def normal_values(rng, dims, deviation, limit, pieces=(), kind=jnp.bfloat16):
    result = deviation * jax.random.normal(rng, dims, jnp.float32)
    if pieces:
        result = result * levels(rng, dims, pieces, -0.22, 0.18)
    return jnp.clip(result, -limit, limit).astype(kind)


def setup_inputs(seed: int = 0) -> dict:
    key_of = jax.random.split(jax.random.key(seed), 9)
    images = normal_values(key_of[0], (BATCH, HEIGHT, COLS, CHANS), 1.0, 6.0, ((0, 2), (1, 16)))
    cotangent = draw_cotangent(jax.random.fold_in(key_of[8], 71), 0)
    pointwise = normal_values(key_of[2], (SLOTS, CHANS, CHANS), CHANS ** -0.5, 0.1875, ((0, 4),))
    depthwise = normal_values(key_of[3], (SLOTS, 9, CHANS), 9 ** -0.5, 2.0, ((0, 4),), jnp.float32)
    norm_gain = jnp.clip(1.0 + 0.15 * jax.random.normal(key_of[4], (SLOTS, CHANS), jnp.float32), 0.25, 1.75)
    norm_shift = normal_values(key_of[5], (SLOTS, CHANS), 0.3, 1.75, ((0, 4),), jnp.float32)
    cell_counts = draw_cell_counts(jax.random.fold_in(key_of[8], 71), 0)
    dilations = draw_dilations(jax.random.fold_in(key_of[8], 71), 0)
    return dict(images=images, cotangent=cotangent, pointwise=pointwise, depthwise=depthwise, norm_gain=norm_gain, norm_shift=norm_shift, cell_counts=cell_counts, dilations=dilations)


EPSILON = 1e-05

def tap_sum(padded, kernel, dilation, sign_step, row_count, col_count):
    row_axis = padded.ndim - 3
    running = jnp.zeros(padded.shape[:row_axis] + (row_count, col_count, padded.shape[-1]), jnp.float32)
    for row_tap in range(3):
        for col_tap in range(3):
            row_anchor = (DMAX + sign_step * (row_tap - 1) * dilation).astype(jnp.int32)
            col_anchor = (DMAX + sign_step * (col_tap - 1) * dilation).astype(jnp.int32)
            window = lax.dynamic_slice_in_dim(padded, row_anchor, row_count, row_axis)
            window = lax.dynamic_slice_in_dim(window, col_anchor, col_count, row_axis + 1)
            running = running + window.astype(jnp.float32) * kernel[3 * row_tap + col_tap]
    return running

def pad_both(tensor):
    widths = [(0, 0)] * (tensor.ndim - 3) + [(DMAX, DMAX), (DMAX, DMAX), (0, 0)]
    return jnp.pad(tensor, widths)

def row_blocks(tensor):
    shaped = tensor.reshape(N_DP, MICRO, IMG, N_ROWS, ROWS_DEV, COLS, CHANS)
    return lax.optimization_barrier(jnp.sum(shaped, axis=(1, 2, 4, 5)))

def settle(partial_value, active):
    partial_value = jnp.where(active, partial_value, 0.0)
    rounded = lax.optimization_barrier(partial_value.astype(jnp.bfloat16)).astype(jnp.float32)
    return lax.optimization_barrier(jnp.sum(rounded, axis=(0, 1)))

def cell_forward(current, weights, kernel, gain, shift, dilation):
    population = IMG * HEIGHT * COLS
    wide_input = current.astype(jnp.float32)
    center = lax.optimization_barrier(jnp.sum(wide_input, axis=(2, 3, 4), keepdims=True)) / population
    spread = lax.optimization_barrier(jnp.sum(wide_input * wide_input, axis=(2, 3, 4), keepdims=True)) / population - center * center
    scaling = lax.rsqrt(spread + EPSILON)
    normed = (wide_input - center) * scaling
    activation = jnp.maximum(normed * gain + shift, 0.0).astype(jnp.bfloat16)
    padded = pad_both(activation)
    hidden = tap_sum(padded, kernel, dilation, 1, HEIGHT, COLS).astype(jnp.bfloat16)
    mixed_rows = jnp.dot(hidden.reshape(-1, CHANS), weights, preferred_element_type=jnp.float32)
    outcome = (wide_input + mixed_rows.reshape(current.shape)).astype(jnp.bfloat16)
    return (outcome, (current, padded, hidden, center, scaling))

def cell_backward(gradient, saved_state, weights, kernel, gain, shift, dilation):
    current, padded, hidden, center, scaling = saved_state
    population = IMG * HEIGHT * COLS
    grad_hidden = lax.dot_general(gradient.reshape(-1, CHANS), weights, (((1,), (1,)), ((), ())), preferred_element_type=jnp.float32)
    grad_hidden = grad_hidden.reshape(gradient.shape).astype(jnp.bfloat16)
    grad_act = tap_sum(pad_both(grad_hidden), kernel, dilation, -1, HEIGHT, COLS)
    wide_input = current.astype(jnp.float32)
    normed = (wide_input - center) * scaling
    pre_act = normed * gain + shift
    grad_pre = jnp.where(pre_act > 0, grad_act, 0.0)
    total_a = lax.optimization_barrier(jnp.sum(grad_pre, axis=(2, 3, 4), keepdims=True))
    total_b = lax.optimization_barrier(jnp.sum(grad_pre * normed, axis=(2, 3, 4), keepdims=True))
    grad_input = gradient.astype(jnp.float32) + scaling * gain * (grad_pre - total_a / population - normed * total_b / population)
    grad_input = grad_input.astype(jnp.bfloat16)
    tap_terms = []
    wide_grad = grad_hidden.astype(jnp.float32)
    for row_tap in range(3):
        for col_tap in range(3):
            row_anchor = (DMAX + (row_tap - 1) * dilation).astype(jnp.int32)
            col_anchor = (DMAX + (col_tap - 1) * dilation).astype(jnp.int32)
            window = lax.dynamic_slice_in_dim(padded, row_anchor, HEIGHT, 3)
            window = lax.dynamic_slice_in_dim(window, col_anchor, COLS, 4)
            tap_terms.append(row_blocks(window.astype(jnp.float32) * wide_grad))
    small_terms = jnp.concatenate([jnp.stack(tap_terms, axis=2), row_blocks(grad_pre * normed)[:, :, None], row_blocks(grad_pre)[:, :, None]], axis=2)
    hidden_rows = hidden.astype(jnp.float32).reshape(N_DP, MICRO, IMG, N_ROWS, ROWS_DEV, COLS, CHANS)
    grad_rows = gradient.astype(jnp.float32).reshape(N_DP, MICRO, IMG, N_ROWS, ROWS_DEV, COLS, CHANS)
    weight_part = jnp.einsum('rmaqhwc,rmaqhwd->rqcd', hidden_rows, grad_rows)
    return (grad_input, weight_part, small_terms)

def reference(images, cotangent, pointwise, depthwise, norm_gain, norm_shift, cell_counts, dilations):
    full_shape = (N_DP, MICRO, IMG, HEIGHT, COLS, CHANS)
    current = images.reshape(full_shape)
    saved = []
    sections = []
    for phase_num in range(SEGMENTS):
        for slot_num in range(CMAX):
            cell_index = phase_num * CMAX + slot_num
            active = slot_num < cell_counts[phase_num]
            outcome, saved_state = cell_forward(current, pointwise[cell_index], depthwise[cell_index], norm_gain[cell_index], norm_shift[cell_index], dilations[cell_index])
            saved.append((saved_state, active))
            current = jnp.where(active, outcome, current)
        sections.append(current.reshape(BATCH, HEIGHT, COLS, CHANS))
    gradient = cotangent.reshape(full_shape)
    grad_weights = [None] * SLOTS
    grad_smalls = [None] * SLOTS
    for cell_index in reversed(range(SLOTS)):
        saved_state, active = saved[cell_index]
        grad_input, weight_part, small_terms = cell_backward(gradient, saved_state, pointwise[cell_index], depthwise[cell_index], norm_gain[cell_index], norm_shift[cell_index], dilations[cell_index])
        grad_weights[cell_index] = settle(weight_part, active)
        grad_smalls[cell_index] = settle(small_terms, active)
        gradient = jnp.where(active, grad_input, gradient)
    smalls = jnp.stack(grad_smalls)
    return (jnp.stack(sections), jnp.stack(grad_weights), smalls[:, :9], smalls[:, 9:])
```

```python
import functools

import jax
import jax.numpy as jnp
from jax import lax
from jax.experimental import pallas as pl
from jax.experimental.pallas import tpu as pltpu
from jax.sharding import PartitionSpec as P

DMAX = 2
MICRO = 2
IMG = 2
EPSILON = 1e-05
MESH = pl.DeviceIdType.MESH
LANES = 128
SUB = 8
F32 = jnp.float32
BF16 = jnp.bfloat16


def window_kernel(
    geo,
    x_ref,
    cot_ref,
    w_hbm,
    par_ref,
    act_ref,
    dil_ref,
    sec_out,
    hid_out,
    grad_out,
    small_out,
    wv,
    xs,
    xpos,
    apos,
    hpos,
    ghpos,
    gppos,
    gpos,
    gnat,
    hs,
    gs,
    gpn,
    gph,
    coth,
    stat_own,
    stat_in,
    norms,
    small,
    sec_in,
    hid_in,
    grad_in,
    small_in,
    w_sem,
    stat_ss,
    stat_rs,
    halo_ss,
    halo_rs,
    own_ss,
    own_rs,
    copy_sem,
):
    slots, segs, row_devs, local_rows, cols, chans = geo
    per = slots // segs
    half = segs // MICRO
    group = half * row_devs
    pos = local_rows * cols
    groups = chans // LANES
    wide = cols + 2 * DMAX
    chunks = cols // SUB
    population = IMG * local_rows * row_devs * cols
    seg = lax.axis_index("segment")
    row = lax.axis_index("rows")
    micro = seg // half
    gid = (seg % half) * row_devs + row
    up = (row + row_devs - 1) % row_devs
    down = (row + 1) % row_devs
    has_up = row > 0
    has_down = row < row_devs - 1

    def peer(k):
        other = (gid + k) % group
        return {"segment": micro * half + other // row_devs, "rows": other % row_devs}

    def greet(k, carry):
        pl.semaphore_signal(barrier, inc=1, device_id=peer(k), device_id_type=MESH)
        return carry

    for j in range(slots):
        pltpu.make_async_copy(w_hbm.at[j], wv.at[j], w_sem.at[j]).start()

    barrier = pltpu.get_barrier_semaphore()
    lax.fori_loop(1, group, greet, 0)
    outside = segs - half
    for k in range(outside):
        other = (micro * half + half + k) % segs
        pl.semaphore_signal(barrier, inc=1, device_id={"segment": other}, device_id_type=MESH)
    pl.semaphore_wait(barrier, group - 1 + outside)

    def halo_sends(step, src, up_dst, down_dst):
        a = pltpu.make_async_remote_copy(
            src, up_dst, halo_ss.at[step, 0], halo_rs.at[step, 0],
            device_id={"rows": up}, device_id_type=MESH)
        b = pltpu.make_async_remote_copy(
            src, down_dst, halo_ss.at[step, 1], halo_rs.at[step, 1],
            device_id={"rows": down}, device_id_type=MESH)
        return a, b

    def cot_sends():
        return halo_sends(2 * slots, cot_ref, coth.at[1], coth.at[0])

    def fwd_sends(j):
        return halo_sends(j, xs.at[j, 1], xs.at[j, 2], xs.at[j, 0])

    def bwd_sends(j):
        return halo_sends(slots + j, gpn.at[j], gph.at[j, 1], gph.at[j, 0])

    def stat_send(step, k):
        return pltpu.make_async_remote_copy(
            stat_own.at[step], stat_in.at[step, k - 1], stat_ss.at[step], stat_rs.at[step],
            device_id=peer(k), device_id_type=MESH)

    def push_stats(step):
        def body(k, carry):
            stat_send(step, k).start()
            return carry
        lax.fori_loop(1, group, body, 0)

    def stats_whole(step):
        return pltpu.make_async_remote_copy(
            stat_in.at[step], stat_in.at[step], stat_ss.at[step], stat_rs.at[step],
            device_id=peer(1), device_id_type=MESH)

    def to_owner(src, dst, slot, kind, owner):
        return pltpu.make_async_remote_copy(
            src, dst, own_ss.at[slot, kind], own_rs.at[slot % per, kind],
            device_id={"segment": owner}, device_id_type=MESH)

    def give(src, dst, slot, kind, owner):
        @pl.when(seg != owner)
        def _():
            to_owner(src, dst, slot, kind, owner).start()

        @pl.when(seg == owner)
        def _():
            pltpu.make_async_copy(src, dst, copy_sem.at[slot, kind]).start()

    def given(src, dst, slot, kind, owner):
        @pl.when(seg != owner)
        def _():
            to_owner(src, dst, slot, kind, owner).wait_send()

        @pl.when(seg == owner)
        def _():
            pltpu.make_async_copy(src, dst, copy_sem.at[slot, kind]).wait()

    def hid_args(j):
        return hs.at[j], hid_in.at[j % per, (seg - j // per + segs) % segs], j, 0, j // per

    def grad_args(j):
        return gs.at[j], grad_in.at[j % per, (seg - j // per + segs) % segs], j, 1, j // per

    def small_args(j):
        return small.at[j], small_in.at[j % per, (seg - j // per + segs) % segs], j, 2, j // per

    def sec_args(j):
        return xs.at[j + 1, 1], sec_in.at[seg], j, 3, j // per

    for a in cot_sends():
        a.start()

    xs[0, 1] = x_ref[...]

    edge = jnp.zeros((DMAX * SUB, LANES), F32)

    def clear(j, carry):
        for r in range(3 * local_rows):
            apos[j, pl.ds(r * wide * SUB, DMAX * SUB), :] = edge
            apos[j, pl.ds((r * wide + DMAX + cols) * SUB, DMAX * SUB), :] = edge
        return carry

    lax.fori_loop(0, slots, clear, 0)
    for r in range(3 * local_rows):
        ghpos[pl.ds(r * wide * SUB, DMAX * SUB), :] = edge
        ghpos[pl.ds((r * wide + DMAX + cols) * SUB, DMAX * SUB), :] = edge

    def param(j, t):
        return par_ref[j, pl.ds(t * SUB, SUB), :]

    def tiles(value):
        return value.reshape(value.shape[0] // SUB, SUB, LANES)

    def flat(value):
        return value.reshape(-1, LANES)

    def spread_out(src, dst, base):
        for g in range(groups):
            dst[pl.ds(base * SUB + g, pos, stride=SUB), :] = src[:, g * LANES : (g + 1) * LANES].astype(F32)

    def own_rows(chunk):
        return chunk // chunks, chunk % chunks

    def at(p):
        return pl.ds(pl.multiple_of(p * SUB, SUB), SUB * SUB)

    def row_ok(value, r):
        if r < local_rows:
            return jnp.where(has_up, value, 0.0)
        if r >= 2 * local_rows:
            return jnp.where(has_down, value, 0.0)
        return value

    zero = jnp.zeros((SUB, LANES), F32)

    def reach(ref, lead, r, c, two):
        found = []
        for a in (-1, 0, 1):
            for b in (-1, 0, 1):
                both = [
                    tiles(ref[lead + (at((r + a * d) * wide + DMAX + c * SUB + b * d), slice(None))])
                    for d in ((1, 2) if a or b else (1,))
                ]
                found.append(jnp.where(two, both[1], both[0]) if len(both) > 1 else both[0])
        return found

    def switch(ref, j, shape):
        return jnp.full(shape, ref[j], F32) > 0.5

    def forward(j, carry):
        spread_out(xs.at[j, 1], xpos.at[j], pos)

        def sums(chunk, acc):
            v = tiles(xpos[j, at(pos + chunk * SUB), :])
            return acc[0] + jnp.sum(v, axis=0), acc[1] + jnp.sum(v * v, axis=0)

        s1, s2 = lax.fori_loop(0, pos // SUB, sums, (zero, zero))
        stat_own[j, 0:SUB, :] = s1
        stat_own[j, SUB : 2 * SUB, :] = s2
        push_stats(j)
        for a in fwd_sends(j):
            a.start()
        stats_whole(j).wait_recv()
        total = jnp.sum(stat_in[j], axis=0) + stat_own[j]
        center = total[0:SUB] / population
        spread = total[SUB : 2 * SUB] / population - center * center
        scaling = lax.rsqrt(spread + EPSILON)
        norms[j, 0:SUB, :] = center
        norms[j, SUB : 2 * SUB, :] = scaling
        gain = param(j, 9)
        shift = param(j, 10)

        def activate(r):
            def body(chunk, carry):
                v = tiles(xpos[j, at(r * cols + chunk * SUB), :])
                v = jnp.maximum((v - center) * scaling * gain + shift, 0.0)
                v = row_ok(v, r).astype(BF16).astype(F32)
                apos[j, at(r * wide + DMAX + chunk * SUB), :] = flat(v)
                return carry
            lax.fori_loop(0, chunks, body, 0)

        for r in range(local_rows, 2 * local_rows):
            activate(r)
        for side in range(2):
            fwd_sends(j)[side].wait_recv()
        spread_out(xs.at[j, 0], xpos.at[j], 0)
        spread_out(xs.at[j, 2], xpos.at[j], 2 * pos)
        for r in range(local_rows):
            activate(r)
            activate(2 * local_rows + r)
        two = switch(dil_ref, j, (SUB, SUB, LANES))
        taps = [param(j, t) for t in range(9)]

        def mix(chunk, carry):
            r, c = own_rows(chunk)
            acc = jnp.zeros((SUB, SUB, LANES), F32)
            for v, tap in zip(reach(apos, (j,), local_rows + r, c, two), taps):
                acc = acc + v * tap
            hpos[at(chunk * SUB), :] = flat(acc)
            return carry

        lax.fori_loop(0, pos // SUB, mix, 0)
        for g in range(groups):
            hs[j, :, g * LANES : (g + 1) * LANES] = hpos[pl.ds(g, pos, stride=SUB), :].astype(BF16)
        give(*hid_args(j))
        pltpu.make_async_copy(w_hbm.at[j], wv.at[j], w_sem.at[j]).wait()
        step = chans // 4
        active = switch(act_ref, j, (pos, step))
        for n in range(4):
            cut = slice(n * step, (n + 1) * step)
            mixed = jnp.dot(hs[j], wv[j, :, cut], preferred_element_type=F32)
            old = xs[j, 1, :, cut].astype(F32)
            xs[j + 1, 1, :, cut] = jnp.where(active, old + mixed, old).astype(BF16)

        @pl.when(j % per == per - 1)
        def _():
            give(*sec_args(j))

        return carry

    lax.fori_loop(0, slots, forward, 0)

    for a in cot_sends():
        a.wait_recv()
    for side, src in enumerate((coth.at[0], cot_ref, coth.at[1])):
        for g in range(groups):
            v = src[:, g * LANES : (g + 1) * LANES].astype(F32)
            v = row_ok(v, side * local_rows)
            gpos[pl.ds(side * pos * SUB + g, pos, stride=SUB), :] = v
            gnat[side * pos : (side + 1) * pos, g * LANES : (g + 1) * LANES] = v.astype(BF16)

    def backward(t, carry):
        j = slots - 1 - t
        step = slots + j
        active = switch(act_ref, j, (SUB, SUB, LANES))
        live = switch(act_ref, j, (SUB, LANES))
        gs[j] = jnp.where(
            switch(act_ref, j, (pos, chans)), gnat[pos : 2 * pos, :].astype(F32), 0.0).astype(BF16)
        give(*grad_args(j))
        width = chans // 4
        for n in range(4):
            gh = lax.dot_general(
                gnat[...], wv[j, n * width : (n + 1) * width, :],
                (((1,), (1,)), ((), ())), preferred_element_type=F32)
            gh = gh.astype(BF16).astype(F32)
            for k in range(width // LANES):
                g = n * (width // LANES) + k
                for r in range(3 * local_rows):
                    ghpos[pl.ds((r * wide + DMAX) * SUB + g, cols, stride=SUB), :] = gh[
                        r * cols : (r + 1) * cols, k * LANES : (k + 1) * LANES]
        two = switch(dil_ref, j, (SUB, SUB, LANES))
        taps = [param(j, k) for k in range(9)]
        gain = param(j, 9)
        shift = param(j, 10)
        center = norms[j, 0:SUB, :]
        scaling = norms[j, SUB : 2 * SUB, :]

        def pull(chunk, acc):
            r, c = own_rows(chunk)
            total = jnp.zeros((SUB, SUB, LANES), F32)
            for v, tap in zip(reach(ghpos, (), local_rows + r, c, two), taps[::-1]):
                total = total + v * tap
            normed = (tiles(xpos[j, at(pos + chunk * SUB), :]) - center) * scaling
            total = jnp.where(normed * gain + shift > 0, total, 0.0)
            gppos[at(pos + chunk * SUB), :] = flat(total)
            return acc[0] + jnp.sum(total, axis=0), acc[1] + jnp.sum(total * normed, axis=0)

        sum_a, sum_b = lax.fori_loop(0, pos // SUB, pull, (zero, zero))
        stat_own[step, 0:SUB, :] = sum_a
        stat_own[step, SUB : 2 * SUB, :] = sum_b

        @pl.when(j > 0)
        def _():
            push_stats(step)
            for g in range(groups):
                gpn[j, :, g * LANES : (g + 1) * LANES] = gppos[
                    pl.ds(pos * SUB + g, pos, stride=SUB), :].astype(BF16)
            for a in bwd_sends(j):
                a.start()

        def tap_grads(chunk, acc):
            r, c = own_rows(chunk)
            gh = tiles(ghpos[at((local_rows + r) * wide + DMAX + c * SUB), :])
            found = reach(apos, (j,), local_rows + r, c, two)
            return tuple(t + jnp.sum(v * gh, axis=0) for t, v in zip(acc, found))

        terms = lax.fori_loop(0, pos // SUB, tap_grads, (zero,) * 9)
        for k, term in enumerate(terms + (sum_b, sum_a)):
            small[j, k * SUB : (k + 1) * SUB, :] = jnp.where(live, term, 0.0)
        give(*small_args(j))

        @pl.when(j > 0)
        def _():
            stats_whole(step).wait_recv()
            total = jnp.sum(stat_in[step], axis=0) + stat_own[step]
            mean_a = total[0:SUB] / population
            mean_b = total[SUB : 2 * SUB] / population
            for side in range(2):
                bwd_sends(j)[side].wait_recv()
            spread_out(gph.at[j, 0], gppos, 0)
            spread_out(gph.at[j, 1], gppos, 2 * pos)
            factor = scaling * gain
            for r in range(3 * local_rows):
                def body(chunk, carry):
                    where = at(r * cols + chunk * SUB)
                    normed = (tiles(xpos[j, where, :]) - center) * scaling
                    old = tiles(gpos[where, :])
                    new = old + factor * (tiles(gppos[where, :]) - mean_a - normed * mean_b)
                    new = row_ok(jnp.where(active, new, old), r).astype(BF16).astype(F32)
                    gpos[where, :] = flat(new)
                    return carry
                lax.fori_loop(0, chunks, body, 0)
            for g in range(groups):
                gnat[:, g * LANES : (g + 1) * LANES] = gpos[pl.ds(g, 3 * pos, stride=SUB), :].astype(BF16)

        return carry

    lax.fori_loop(0, slots, backward, 0)

    def finish(j, carry):
        given(*hid_args(j))
        given(*grad_args(j))
        given(*small_args(j))
        for a in fwd_sends(j):
            a.wait_send()
        stats_whole(j).wait_send()

        @pl.when(j % per == per - 1)
        def _():
            given(*sec_args(j))

        @pl.when(j > 0)
        def _():
            for a in bwd_sends(j):
                a.wait_send()
            stats_whole(slots + j).wait_send()

        return carry

    lax.fori_loop(0, slots, finish, 0)
    for a in cot_sends():
        a.wait_send()

    def landed(dst, slot, kind):
        to_owner(dst, dst, slot, kind, (seg + 1) % segs).wait_recv()

    for k in range(per):
        landed(hid_in.at[k, pl.ds(1, segs - 1)], k, 0)
        landed(grad_in.at[k, pl.ds(1, segs - 1)], k, 1)
        landed(small_in.at[k, pl.ds(1, segs - 1)], k, 2)
    landed(sec_in.at[pl.ds(1, segs - 1)], per - 1, 3)
    sec_out[...] = sec_in[...]
    hid_out[...] = hid_in[...]
    grad_out[...] = grad_in[...]
    small_out[...] = jnp.sum(small_in[...], axis=1)


def run_window(geo, x, cot, weights, params, active, dilations):
    slots, segs, row_devs, local_rows, cols, chans = geo
    per = slots // segs
    pos = local_rows * cols
    group = segs // MICRO * row_devs
    wide = cols + 2 * DMAX
    ext = 3 * local_rows * wide * SUB
    vm = pltpu.VMEM
    dma = pltpu.SemaphoreType.DMA
    vmem = pl.BlockSpec(memory_space=pltpu.VMEM)
    smem = pl.BlockSpec(memory_space=pltpu.SMEM)
    return pl.pallas_call(
        functools.partial(window_kernel, geo),
        out_shape=(
            jax.ShapeDtypeStruct((segs, pos, chans), BF16),
            jax.ShapeDtypeStruct((per, segs, pos, chans), BF16),
            jax.ShapeDtypeStruct((per, segs, pos, chans), BF16),
            jax.ShapeDtypeStruct((per, 11 * SUB, LANES), F32),
        ),
        in_specs=[vmem, vmem, pl.BlockSpec(memory_space=pl.ANY), vmem, smem, smem],
        out_specs=(vmem,) * 4,
        scratch_shapes=[
            vm((slots, chans, chans), BF16),
            vm((slots + 1, 3, pos, chans), BF16),
            vm((slots, 3 * pos * SUB, LANES), F32),
            vm((slots, ext, LANES), F32),
            vm((pos * SUB, LANES), F32),
            vm((ext, LANES), F32),
            vm((3 * pos * SUB, LANES), F32),
            vm((3 * pos * SUB, LANES), F32),
            vm((3 * pos, chans), BF16),
            vm((slots, pos, chans), BF16),
            vm((slots, pos, chans), BF16),
            vm((slots, pos, chans), BF16),
            vm((slots, 2, pos, chans), BF16),
            vm((2, pos, chans), BF16),
            vm((2 * slots, 2 * SUB, LANES), F32),
            vm((2 * slots, group - 1, 2 * SUB, LANES), F32),
            vm((slots, 2 * SUB, LANES), F32),
            vm((slots, 11 * SUB, LANES), F32),
            vm((segs, pos, chans), BF16),
            vm((per, segs, pos, chans), BF16),
            vm((per, segs, pos, chans), BF16),
            vm((per, segs, 11 * SUB, LANES), F32),
            dma((slots,)),
            dma((2 * slots,)),
            dma((2 * slots,)),
            dma((2 * slots + 1, 2)),
            dma((2 * slots + 1, 2)),
            dma((slots, 4)),
            dma((per, 4)),
            dma((slots, 4)),
        ],
        compiler_params=pltpu.CompilerParams(
            collective_id=0, has_side_effects=True, vmem_limit_bytes=64000 * 1024),
        name="window",
    )(x, cot, weights, params, active, dilations)


def local(images, cotangent, pointwise, depthwise, norm_gain, norm_shift, cell_counts, dilations):
    segs = lax.axis_size("segment")
    row_devs = lax.axis_size("rows")
    dps = lax.axis_size("dp")
    seg = lax.axis_index("segment")
    per, chans = pointwise.shape[0], pointwise.shape[2]
    count, local_rows, cols, _ = images.shape
    slots = per * segs
    pos = local_rows * cols
    geo = (slots, segs, row_devs, local_rows, cols, chans)
    x = lax.dynamic_index_in_dim(images.reshape(count, pos, chans), seg, 0, keepdims=False)
    cot = lax.dynamic_index_in_dim(cotangent.reshape(count, pos, chans), seg, 0, keepdims=False)
    part = chans // dps
    mine = lax.dynamic_slice_in_dim(pointwise, lax.axis_index("dp") * part, part, 1)
    weights = lax.all_gather(mine, "segment", axis=0, tiled=True)
    weights = lax.all_gather(weights, "dp", axis=1, tiled=True)
    flags = (jnp.arange(per, dtype=jnp.int32) < cell_counts[0]).astype(F32)
    pack = jnp.concatenate(
        [depthwise, norm_gain[:, None], norm_shift[:, None],
         jnp.broadcast_to(flags[:, None, None], (per, 1, chans)),
         jnp.broadcast_to((dilations > 1).astype(F32)[:, None, None], (per, 1, chans))], axis=1)
    pack = lax.all_gather(pack, "segment", axis=0, tiled=True)
    active = pack[:, 11, 0]
    rates = pack[:, 12, 0]
    params = pack[:, :11].reshape(slots, 11 * SUB, LANES)
    sec, hid, grad, small = run_window(geo, x, cot, weights, params, active, rates)
    hid = hid.reshape(per, segs * pos, chans)
    grad = grad.reshape(per, segs * pos, chans)
    part_w = lax.dot_general(hid, grad, (((1,), (1,)), ((0,), (0,))), preferred_element_type=F32)
    small = jnp.swapaxes(small.reshape(per, 11, chans), 1, 2)
    small = jnp.pad(small, ((0, 0), (0, 0), (0, LANES - 11)))
    both = jnp.concatenate([part_w.astype(BF16), small.astype(BF16)], axis=2)
    both = lax.psum_scatter(both, ("dp", "rows"), scatter_dimension=1, tiled=True).astype(F32)
    grad_small = jnp.swapaxes(both[:, :, chans : chans + 11], 1, 2)
    return (
        sec.reshape(1, count, local_rows, cols, chans),
        both[:, :, :chans],
        grad_small[:, :9],
        grad_small[:, 9:],
    )


def solution(mesh):
    return jax.shard_map(
        local,
        mesh=mesh,
        in_specs=(
            P("dp", "rows", None, None),
            P("dp", "rows", None, None),
            P("segment", None, None),
            P("segment", None, None),
            P("segment", None),
            P("segment", None),
            P("segment"),
            P("segment"),
        ),
        out_specs=(
            P("segment", "dp", "rows", None, None),
            P("segment", ("dp", "rows"), None),
            P("segment", None, ("dp", "rows")),
            P("segment", None, ("dp", "rows")),
        ),
        check_vma=False,
    )
```

```python
import functools

import jax
import jax.numpy as jnp
from jax import lax
from jax.experimental import pallas as pl
from jax.experimental.pallas import tpu as pltpu
from jax.sharding import PartitionSpec as P

DMAX = 2
MICRO = 2
IMG = 2
EPSILON = 1e-05
MESH = pl.DeviceIdType.MESH
LANES = 128
SUB = 8
F32 = jnp.float32
BF16 = jnp.bfloat16


def window_kernel(
    geo,
    x_ref,
    cot_ref,
    w_hbm,
    par_ref,
    act_ref,
    dil_ref,
    sec_out,
    weight_out,
    small_out,
    wv,
    xs,
    xpos,
    apos,
    hpos,
    ghpos,
    gppos,
    gpos,
    gnat,
    hs,
    gs,
    gpn,
    gph,
    coth,
    stat_own,
    stat_mid,
    near_in,
    far_in,
    norms,
    small,
    sec_in,
    hid_in,
    grad_in,
    small_in,
    twin_out,
    twin_in,
    half_sum,
    share_in,
    tiny,
    tiny_in,
    w_sem,
    near_ss,
    near_rs,
    far_ss,
    far_rs,
    twin_ss,
    twin_rs,
    share_ss,
    share_rs,
    tiny_ss,
    tiny_rs,
    halo_ss,
    halo_rs,
    own_ss,
    own_rs,
    copy_sem,
):
    slots, segs, row_devs, local_rows, cols, chans, dps = geo
    per = slots // segs
    half = segs // MICRO
    ring = min(4, row_devs)
    lines = row_devs // ring
    far = half * lines
    plane = dps * row_devs
    piece = chans // plane
    part = chans // dps
    pos = local_rows * cols
    groups = chans // LANES
    wide = cols + 2 * DMAX
    chunks = cols // SUB
    population = IMG * local_rows * row_devs * cols
    seg = lax.axis_index("segment")
    row = lax.axis_index("rows")
    micro = seg // half
    core = lax.axis_index("dp")
    line = row // ring
    place = row % ring
    up = (row + row_devs - 1) % row_devs
    down = (row + 1) % row_devs
    has_up = row > 0
    has_down = row < row_devs - 1

    def near_peer(k):
        return {"rows": line * ring + (place + k) % ring}

    def far_peer(k):
        other = ((seg % half) * lines + line + k) % far
        return {"segment": micro * half + other // lines, "rows": other % lines * ring + place}

    def plane_index(k):
        return (core * row_devs + row + k) % plane

    def plane_peer(k):
        other = plane_index(k)
        return {"dp": other // row_devs, "rows": other % row_devs}

    def greet(k, carry):
        pl.semaphore_signal(barrier, inc=1, device_id=plane_peer(k), device_id_type=MESH)
        return carry

    for j in range(slots):
        pltpu.make_async_copy(w_hbm.at[j // per, :, j % per], wv.at[j], w_sem.at[j]).start()

    barrier = pltpu.get_barrier_semaphore()
    lax.fori_loop(1, plane, greet, 0)
    for k in range(1, segs):
        pl.semaphore_signal(
            barrier, inc=1, device_id={"segment": (seg + k) % segs}, device_id_type=MESH)
    for k in range(1, far):
        if k % lines:
            other = (((seg % half) * lines + line + k) % far) // lines

            @pl.when(other != seg % half)
            def _():
                pl.semaphore_signal(barrier, inc=1, device_id=far_peer(k), device_id_type=MESH)
    pl.semaphore_wait(barrier, plane - 1 + segs - 1 + (half - 1) * (lines - 1))

    def halo_sends(step, src, up_dst, down_dst):
        a = pltpu.make_async_remote_copy(
            src, up_dst, halo_ss.at[step, 0], halo_rs.at[step, 0],
            device_id={"rows": up}, device_id_type=MESH)
        b = pltpu.make_async_remote_copy(
            src, down_dst, halo_ss.at[step, 1], halo_rs.at[step, 1],
            device_id={"rows": down}, device_id_type=MESH)
        return a, b

    def cot_sends():
        return halo_sends(2 * slots, cot_ref, coth.at[1], coth.at[0])

    def fwd_sends(j):
        return halo_sends(j, xs.at[j, 1], xs.at[j, 2], xs.at[j, 0])

    def bwd_sends(j):
        return halo_sends(slots + j, gpn.at[j], gph.at[j, 1], gph.at[j, 0])

    def near_send(step, k):
        return pltpu.make_async_remote_copy(
            stat_own.at[step], near_in.at[step, k - 1], near_ss.at[step], near_rs.at[step],
            device_id=near_peer(k), device_id_type=MESH)

    def far_send(step, k):
        return pltpu.make_async_remote_copy(
            stat_mid.at[step], far_in.at[step, k - 1], far_ss.at[step], far_rs.at[step],
            device_id=far_peer(k), device_id_type=MESH)

    def near_all(step):
        return pltpu.make_async_remote_copy(
            near_in.at[step], near_in.at[step], near_ss.at[step], near_rs.at[step],
            device_id=near_peer(1), device_id_type=MESH)

    def far_all(step):
        return pltpu.make_async_remote_copy(
            far_in.at[step], far_in.at[step], far_ss.at[step], far_rs.at[step],
            device_id=far_peer(1), device_id_type=MESH)

    def push_stats(step):
        for k in range(1, ring):
            near_send(step, k).start()

    def total_stats(step):
        near_all(step).wait_recv()
        mid = stat_own[step]
        for k in range(ring - 1):
            mid = mid + near_in[step, k]
        stat_mid[step] = mid
        for k in range(1, far):
            far_send(step, k).start()
        far_all(step).wait_recv()
        for k in range(far - 1):
            mid = mid + far_in[step, k]
        return mid

    def sent_stats(step):
        near_all(step).wait_send()
        far_all(step).wait_send()

    def to_owner(src, dst, slot, kind, owner):
        return pltpu.make_async_remote_copy(
            src, dst, own_ss.at[slot, kind], own_rs.at[slot % per, kind],
            device_id={"segment": owner}, device_id_type=MESH)

    def give(src, dst, slot, kind, owner):
        @pl.when(seg != owner)
        def _():
            to_owner(src, dst, slot, kind, owner).start()

        @pl.when(seg == owner)
        def _():
            pltpu.make_async_copy(src, dst, copy_sem.at[slot, kind]).start()

    def given(src, dst, slot, kind, owner):
        @pl.when(seg != owner)
        def _():
            to_owner(src, dst, slot, kind, owner).wait_send()

        @pl.when(seg == owner)
        def _():
            pltpu.make_async_copy(src, dst, copy_sem.at[slot, kind]).wait()

    def hid_args(j):
        return hs.at[j], hid_in.at[j % per, (seg - j // per + segs) % segs], j, 0, j // per

    def grad_args(j):
        return gs.at[j], grad_in.at[j % per, (seg - j // per + segs) % segs], j, 1, j // per

    def small_args(j):
        return small.at[j], small_in.at[j % per, (seg - j // per + segs) % segs], j, 2, j // per

    def sec_args(j):
        return xs.at[j + 1, 1], sec_in.at[seg], j, 3, j // per

    for a in cot_sends():
        a.start()

    xs[0, 1] = x_ref[...]

    edge = jnp.zeros((DMAX * SUB, LANES), F32)

    def clear(j, carry):
        for r in range(3 * local_rows):
            apos[j, pl.ds(r * wide * SUB, DMAX * SUB), :] = edge
            apos[j, pl.ds((r * wide + DMAX + cols) * SUB, DMAX * SUB), :] = edge
        return carry

    lax.fori_loop(0, slots, clear, 0)
    for r in range(3 * local_rows):
        ghpos[pl.ds(r * wide * SUB, DMAX * SUB), :] = edge
        ghpos[pl.ds((r * wide + DMAX + cols) * SUB, DMAX * SUB), :] = edge

    def param(j, t):
        return par_ref[j, pl.ds(t * SUB, SUB), :]

    def tiles(value):
        return value.reshape(value.shape[0] // SUB, SUB, LANES)

    def flat(value):
        return value.reshape(-1, LANES)

    def spread_out(src, dst, base):
        for g in range(groups):
            dst[pl.ds(base * SUB + g, pos, stride=SUB), :] = src[:, g * LANES : (g + 1) * LANES].astype(F32)

    def own_rows(chunk):
        return chunk // chunks, chunk % chunks

    def at(p):
        return pl.ds(pl.multiple_of(p * SUB, SUB), SUB * SUB)

    def row_ok(value, r):
        if r < local_rows:
            return jnp.where(has_up, value, 0.0)
        if r >= 2 * local_rows:
            return jnp.where(has_down, value, 0.0)
        return value

    zero = jnp.zeros((SUB, LANES), F32)

    def reach(ref, lead, r, c, two):
        found = []
        for a in (-1, 0, 1):
            for b in (-1, 0, 1):
                both = [
                    tiles(ref[lead + (at((r + a * d) * wide + DMAX + c * SUB + b * d), slice(None))])
                    for d in ((1, 2) if a or b else (1,))
                ]
                found.append(jnp.where(two, both[1], both[0]) if len(both) > 1 else both[0])
        return found

    def switch(ref, j, shape):
        return jnp.full(shape, ref[j], F32) > 0.5

    def forward(j, carry):
        spread_out(xs.at[j, 1], xpos.at[j], pos)

        def sums(chunk, acc):
            v = tiles(xpos[j, at(pos + chunk * SUB), :])
            return acc[0] + jnp.sum(v, axis=0), acc[1] + jnp.sum(v * v, axis=0)

        s1, s2 = lax.fori_loop(0, pos // SUB, sums, (zero, zero))
        stat_own[j, 0:SUB, :] = s1
        stat_own[j, SUB : 2 * SUB, :] = s2
        push_stats(j)
        for a in fwd_sends(j):
            a.start()
        total = total_stats(j)
        center = total[0:SUB] / population
        spread = total[SUB : 2 * SUB] / population - center * center
        scaling = lax.rsqrt(spread + EPSILON)
        norms[j, 0:SUB, :] = center
        norms[j, SUB : 2 * SUB, :] = scaling
        gain = param(j, 9)
        shift = param(j, 10)

        def activate(r):
            def body(chunk, carry):
                v = tiles(xpos[j, at(r * cols + chunk * SUB), :])
                v = jnp.maximum((v - center) * scaling * gain + shift, 0.0)
                v = row_ok(v, r).astype(BF16).astype(F32)
                apos[j, at(r * wide + DMAX + chunk * SUB), :] = flat(v)
                return carry
            lax.fori_loop(0, chunks, body, 0)

        for r in range(local_rows, 2 * local_rows):
            activate(r)
        for side in range(2):
            fwd_sends(j)[side].wait_recv()
        spread_out(xs.at[j, 0], xpos.at[j], 0)
        spread_out(xs.at[j, 2], xpos.at[j], 2 * pos)
        for r in range(local_rows):
            activate(r)
            activate(2 * local_rows + r)
        two = switch(dil_ref, j, (SUB, SUB, LANES))
        taps = [param(j, t) for t in range(9)]

        def mix(chunk, carry):
            r, c = own_rows(chunk)
            acc = jnp.zeros((SUB, SUB, LANES), F32)
            for v, tap in zip(reach(apos, (j,), local_rows + r, c, two), taps):
                acc = acc + v * tap
            hpos[at(chunk * SUB), :] = flat(acc)
            return carry

        lax.fori_loop(0, pos // SUB, mix, 0)
        for g in range(groups):
            hs[j, :, g * LANES : (g + 1) * LANES] = hpos[pl.ds(g, pos, stride=SUB), :].astype(BF16)
        give(*hid_args(j))
        pltpu.make_async_copy(w_hbm.at[j // per, :, j % per], wv.at[j], w_sem.at[j]).wait()
        step = chans // 4
        active = switch(act_ref, j, (pos, step))
        for n in range(4):
            cut = slice(n * step, (n + 1) * step)
            mixed = jnp.dot(hs[j], wv[j, :, :, cut].reshape(chans, step), preferred_element_type=F32)
            old = xs[j, 1, :, cut].astype(F32)
            xs[j + 1, 1, :, cut] = jnp.where(active, old + mixed, old).astype(BF16)

        @pl.when(j % per == per - 1)
        def _():
            give(*sec_args(j))

        return carry

    lax.fori_loop(0, slots, forward, 0)

    for a in cot_sends():
        a.wait_recv()
    for side, src in enumerate((coth.at[0], cot_ref, coth.at[1])):
        for g in range(groups):
            v = src[:, g * LANES : (g + 1) * LANES].astype(F32)
            v = row_ok(v, side * local_rows)
            gpos[pl.ds(side * pos * SUB + g, pos, stride=SUB), :] = v
            gnat[side * pos : (side + 1) * pos, g * LANES : (g + 1) * LANES] = v.astype(BF16)

    def backward(t, carry):
        j = slots - 1 - t
        step = slots + j
        active = switch(act_ref, j, (SUB, SUB, LANES))
        live = switch(act_ref, j, (SUB, LANES))
        gs[j] = jnp.where(
            switch(act_ref, j, (pos, chans)), gnat[pos : 2 * pos, :].astype(F32), 0.0).astype(BF16)
        give(*grad_args(j))
        width = chans // 4
        for n in range(4):
            gh = lax.dot_general(
                gnat[...], wv[j].reshape(chans, chans)[n * width : (n + 1) * width],
                (((1,), (1,)), ((), ())), preferred_element_type=F32)
            gh = gh.astype(BF16).astype(F32)
            for k in range(width // LANES):
                g = n * (width // LANES) + k
                for r in range(3 * local_rows):
                    ghpos[pl.ds((r * wide + DMAX) * SUB + g, cols, stride=SUB), :] = gh[
                        r * cols : (r + 1) * cols, k * LANES : (k + 1) * LANES]
        two = switch(dil_ref, j, (SUB, SUB, LANES))
        taps = [param(j, k) for k in range(9)]
        gain = param(j, 9)
        shift = param(j, 10)
        center = norms[j, 0:SUB, :]
        scaling = norms[j, SUB : 2 * SUB, :]

        def pull(chunk, acc):
            r, c = own_rows(chunk)
            total = jnp.zeros((SUB, SUB, LANES), F32)
            for v, tap in zip(reach(ghpos, (), local_rows + r, c, two), taps[::-1]):
                total = total + v * tap
            normed = (tiles(xpos[j, at(pos + chunk * SUB), :]) - center) * scaling
            total = jnp.where(normed * gain + shift > 0, total, 0.0)
            gppos[at(pos + chunk * SUB), :] = flat(total)
            return acc[0] + jnp.sum(total, axis=0), acc[1] + jnp.sum(total * normed, axis=0)

        sum_a, sum_b = lax.fori_loop(0, pos // SUB, pull, (zero, zero))
        stat_own[step, 0:SUB, :] = sum_a
        stat_own[step, SUB : 2 * SUB, :] = sum_b

        @pl.when(j > 0)
        def _():
            push_stats(step)
            for g in range(groups):
                gpn[j, :, g * LANES : (g + 1) * LANES] = gppos[
                    pl.ds(pos * SUB + g, pos, stride=SUB), :].astype(BF16)
            for a in bwd_sends(j):
                a.start()

        def tap_grads(chunk, acc):
            r, c = own_rows(chunk)
            gh = tiles(ghpos[at((local_rows + r) * wide + DMAX + c * SUB), :])
            found = reach(apos, (j,), local_rows + r, c, two)
            return tuple(t + jnp.sum(v * gh, axis=0) for t, v in zip(acc, found))

        terms = lax.fori_loop(0, pos // SUB, tap_grads, (zero,) * 9)
        for k, term in enumerate(terms + (sum_b, sum_a)):
            small[j, k * SUB : (k + 1) * SUB, :] = jnp.where(live, term, 0.0)
        give(*small_args(j))

        @pl.when(j > 0)
        def _():
            total = total_stats(step)
            mean_a = total[0:SUB] / population
            mean_b = total[SUB : 2 * SUB] / population
            for side in range(2):
                bwd_sends(j)[side].wait_recv()
            spread_out(gph.at[j, 0], gppos, 0)
            spread_out(gph.at[j, 1], gppos, 2 * pos)
            factor = scaling * gain
            for r in range(3 * local_rows):
                def body(chunk, carry):
                    where = at(r * cols + chunk * SUB)
                    normed = (tiles(xpos[j, where, :]) - center) * scaling
                    old = tiles(gpos[where, :])
                    new = old + factor * (tiles(gppos[where, :]) - mean_a - normed * mean_b)
                    new = row_ok(jnp.where(active, new, old), r).astype(BF16).astype(F32)
                    gpos[where, :] = flat(new)
                    return carry
                lax.fori_loop(0, chunks, body, 0)
            for g in range(groups):
                gnat[:, g * LANES : (g + 1) * LANES] = gpos[pl.ds(g, 3 * pos, stride=SUB), :].astype(BF16)

        return carry

    lax.fori_loop(0, slots, backward, 0)

    def finish(j, carry):
        given(*hid_args(j))
        given(*grad_args(j))
        given(*small_args(j))
        for a in fwd_sends(j):
            a.wait_send()
        sent_stats(j)

        @pl.when(j % per == per - 1)
        def _():
            given(*sec_args(j))

        @pl.when(j > 0)
        def _():
            for a in bwd_sends(j):
                a.wait_send()
            sent_stats(slots + j)

        return carry

    lax.fori_loop(0, slots, finish, 0)
    for a in cot_sends():
        a.wait_send()

    def landed(dst, slot, kind):
        to_owner(dst, dst, slot, kind, (seg + 1) % segs).wait_recv()

    for k in range(per):
        landed(hid_in.at[k, pl.ds(1, segs - 1)], k, 0)
        landed(grad_in.at[k, pl.ds(1, segs - 1)], k, 1)
        landed(small_in.at[k, pl.ds(1, segs - 1)], k, 2)
    landed(sec_in.at[pl.ds(1, segs - 1)], per - 1, 3)
    sec_out[...] = sec_in[...]

    twin = {"dp": 1 - core}
    block = min(LANES, part)

    def outer(b, first):
        lhs = hid_in[b, :, :, pl.ds(pl.multiple_of(first, block), block)].reshape(segs * pos, block)
        return lax.dot_general(
            lhs, grad_in[b].reshape(segs * pos, chans),
            (((0,), (0,)), ((), ())), preferred_element_type=F32)

    def twin_send(b):
        return pltpu.make_async_remote_copy(
            twin_out.at[b], twin_in.at[b], twin_ss.at[b], twin_rs.at[b],
            device_id=twin, device_id_type=MESH)

    def share_send(b, k):
        other = (row + k) % row_devs
        return pltpu.make_async_remote_copy(
            half_sum.at[b, pl.ds(pl.multiple_of(other * piece, piece), piece)],
            share_in.at[b, k - 1], share_ss.at[b], share_rs.at[b],
            device_id={"rows": other}, device_id_type=MESH)

    def share_all(b):
        return pltpu.make_async_remote_copy(
            share_in.at[b], share_in.at[b], share_ss.at[b], share_rs.at[b],
            device_id={"rows": (row + 1) % row_devs}, device_id_type=MESH)

    def tiny_send(k):
        band = plane_index(k) * groups // plane
        return pltpu.make_async_remote_copy(
            tiny.at[band], tiny_in.at[k - 1], tiny_ss, tiny_rs,
            device_id=plane_peer(k), device_id_type=MESH)

    def tiny_all():
        return pltpu.make_async_remote_copy(
            tiny_in, tiny_in, tiny_ss, tiny_rs, device_id=plane_peer(1), device_id_type=MESH)

    def theirs(b):
        def body(n, carry):
            rows = pl.ds(pl.multiple_of(n * block, block), block)
            twin_out[b, rows, :] = outer(b, (1 - core) * part + n * block).astype(BF16)
            return carry
        lax.fori_loop(0, part // block, body, 0)
        twin_send(b).start()

    def ours(b):
        twin_send(b).wait_recv()

        def body(n, carry):
            rows = pl.ds(pl.multiple_of(n * block, block), block)
            value = outer(b, core * part + n * block) + twin_in[b, rows, :].astype(F32)
            half_sum[b, rows, :] = value.astype(BF16)
            return carry
        lax.fori_loop(0, part // block, body, 0)

        def push(k, carry):
            share_send(b, k).start()
            return carry
        lax.fori_loop(1, row_devs, push, 0)

    for b in range(per):
        theirs(b)
    rows = per * 11
    for b in range(per):
        total = jnp.sum(small_in[b], axis=0)
        gppos[b * 11 * SUB : (b + 1) * 11 * SUB, :] = total
    for g in range(groups):
        tiny[g, 0:rows, :] = gppos[pl.ds(g, rows, stride=SUB), :].astype(BF16)
        tiny[g, rows:, :] = jnp.zeros((32 - rows, LANES), BF16)

    def push_tiny(k, carry):
        tiny_send(k).start()
        return carry

    lax.fori_loop(1, plane, push_tiny, 0)
    for b in range(per):
        ours(b)
    tiny_all().wait_recv()
    small_out[...] = jnp.sum(tiny_in[...].astype(F32), axis=0) + tiny[
        plane_index(0) * groups // plane].astype(F32)
    for b in range(per):
        share_all(b).wait_recv()
        own = half_sum[b, pl.ds(pl.multiple_of(row * piece, piece), piece), :].astype(F32)
        for k in range(row_devs - 1):
            own = own + share_in[b, k].astype(F32)
        weight_out[b] = own
    for b in range(per):
        twin_send(b).wait_send()
        share_all(b).wait_send()
    tiny_all().wait_send()


def run_window(geo, x, cot, weights, params, active, dilations):
    slots, segs, row_devs, local_rows, cols, chans, dps = geo
    per = slots // segs
    pos = local_rows * cols
    ring = min(4, row_devs)
    far = segs // MICRO * (row_devs // ring)
    plane = dps * row_devs
    piece = chans // plane
    part = chans // dps
    wide = cols + 2 * DMAX
    ext = 3 * local_rows * wide * SUB
    vm = pltpu.VMEM
    dma = pltpu.SemaphoreType.DMA
    vmem = pl.BlockSpec(memory_space=pltpu.VMEM)
    smem = pl.BlockSpec(memory_space=pltpu.SMEM)
    return pl.pallas_call(
        functools.partial(window_kernel, geo),
        out_shape=(
            jax.ShapeDtypeStruct((segs, pos, chans), BF16),
            jax.ShapeDtypeStruct((per, piece, chans), F32),
            jax.ShapeDtypeStruct((32, LANES), F32),
        ),
        in_specs=[vmem, vmem, pl.BlockSpec(memory_space=pl.ANY), vmem, smem, smem],
        out_specs=(vmem,) * 3,
        scratch_shapes=[
            vm((slots, plane, piece, chans), BF16),
            vm((slots + 1, 3, pos, chans), BF16),
            vm((slots, 3 * pos * SUB, LANES), F32),
            vm((slots, ext, LANES), F32),
            vm((pos * SUB, LANES), F32),
            vm((ext, LANES), F32),
            vm((3 * pos * SUB, LANES), F32),
            vm((3 * pos * SUB, LANES), F32),
            vm((3 * pos, chans), BF16),
            vm((slots, pos, chans), BF16),
            vm((slots, pos, chans), BF16),
            vm((slots, pos, chans), BF16),
            vm((slots, 2, pos, chans), BF16),
            vm((2, pos, chans), BF16),
            vm((2 * slots, 2 * SUB, LANES), F32),
            vm((2 * slots, 2 * SUB, LANES), F32),
            vm((2 * slots, ring - 1, 2 * SUB, LANES), F32),
            vm((2 * slots, far - 1, 2 * SUB, LANES), F32),
            vm((slots, 2 * SUB, LANES), F32),
            vm((slots, 11 * SUB, LANES), F32),
            vm((segs, pos, chans), BF16),
            vm((per, segs, pos, chans), BF16),
            vm((per, segs, pos, chans), BF16),
            vm((per, segs, 11 * SUB, LANES), F32),
            vm((per, part, chans), BF16),
            vm((per, part, chans), BF16),
            vm((per, part, chans), BF16),
            vm((per, row_devs - 1, piece, chans), BF16),
            vm((chans // LANES, 32, LANES), BF16),
            vm((plane - 1, 32, LANES), BF16),
            dma((slots,)),
            dma((2 * slots,)),
            dma((2 * slots,)),
            dma((2 * slots,)),
            dma((2 * slots,)),
            dma((per,)),
            dma((per,)),
            dma((per,)),
            dma((per,)),
            dma,
            dma,
            dma((2 * slots + 1, 2)),
            dma((2 * slots + 1, 2)),
            dma((slots, 4)),
            dma((per, 4)),
            dma((slots, 4)),
        ],
        compiler_params=pltpu.CompilerParams(
            collective_id=0, has_side_effects=True, vmem_limit_bytes=64000 * 1024),
        name="window",
    )(x, cot, weights, params, active, dilations)


def local(images, cotangent, pointwise, depthwise, norm_gain, norm_shift, cell_counts, dilations):
    segs = lax.axis_size("segment")
    row_devs = lax.axis_size("rows")
    dps = lax.axis_size("dp")
    seg = lax.axis_index("segment")
    per, chans = pointwise.shape[0], pointwise.shape[2]
    count, local_rows, cols, _ = images.shape
    slots = per * segs
    pos = local_rows * cols
    geo = (slots, segs, row_devs, local_rows, cols, chans, dps)
    plane = dps * row_devs
    piece = chans // plane
    index = lax.axis_index("dp") * row_devs + lax.axis_index("rows")
    x = lax.dynamic_index_in_dim(images.reshape(count, pos, chans), seg, 0, keepdims=False)
    cot = lax.dynamic_index_in_dim(cotangent.reshape(count, pos, chans), seg, 0, keepdims=False)
    mine = lax.dynamic_slice_in_dim(pointwise, index * piece, piece, 1)
    weights = lax.all_gather(mine, ("segment", "dp", "rows"))
    weights = weights.reshape(segs, plane, per, piece, chans)
    flags = (jnp.arange(per, dtype=jnp.int32) < cell_counts[0]).astype(F32)
    pack = jnp.concatenate(
        [depthwise, norm_gain[:, None], norm_shift[:, None],
         jnp.broadcast_to(flags[:, None, None], (per, 1, chans)),
         jnp.broadcast_to((dilations > 1).astype(F32)[:, None, None], (per, 1, chans))], axis=1)
    pack = lax.all_gather(pack, "segment", axis=0, tiled=True)
    active = pack[:, 11, 0]
    rates = pack[:, 12, 0]
    params = pack[:, :11].reshape(slots, 11 * SUB, LANES)
    sec, grad_weight, small = run_window(geo, x, cot, weights, params, active, rates)
    small = small[: per * 11].reshape(per, 11, LANES)
    grad_small = lax.dynamic_slice_in_dim(small, index * piece % LANES, min(piece, LANES), 2)
    return (
        sec.reshape(1, count, local_rows, cols, chans),
        grad_weight,
        grad_small[:, :9],
        grad_small[:, 9:],
    )


def solution(mesh):
    return jax.shard_map(
        local,
        mesh=mesh,
        in_specs=(
            P("dp", "rows", None, None),
            P("dp", "rows", None, None),
            P("segment", None, None),
            P("segment", None, None),
            P("segment", None),
            P("segment", None),
            P("segment"),
            P("segment"),
        ),
        out_specs=(
            P("segment", "dp", "rows", None, None),
            P("segment", ("dp", "rows"), None),
            P("segment", None, ("dp", "rows")),
            P("segment", None, ("dp", "rows")),
        ),
        check_vma=False,
    )
```

```python
import functools

import jax
import jax.numpy as jnp
from jax import lax
from jax.experimental import pallas as pl
from jax.experimental.pallas import tpu as pltpu
from jax.sharding import PartitionSpec as P

DMAX = 2
MICRO = 2
IMG = 2
EPSILON = 1e-05
MESH = pl.DeviceIdType.MESH
LANES = 128
SUB = 8
F32 = jnp.float32
BF16 = jnp.bfloat16


def window_kernel(
    geo,
    x_hbm,
    cot_hbm,
    w_hbm,
    pack_ref,
    sec_out,
    weight_out,
    small_out,
    wv,
    xs,
    xpos,
    apos,
    hpos,
    ghpos,
    gppos,
    gpos,
    gnat,
    hs,
    gs,
    gpn,
    gph,
    coth,
    stat_own,
    stat_mid,
    near_in,
    far_in,
    norms,
    small,
    sec_in,
    hid_in,
    grad_in,
    small_in,
    twin_out,
    twin_in,
    half_sum,
    share_in,
    tiny,
    tiny_in,
    par_ref,
    cot_ref,
    in_sem,
    par_ss,
    par_rs,
    x_ss,
    x_rs,
    one_ss,
    one_rs,
    two_ss,
    two_rs,
    mate_ss,
    mate_rs,
    w_sem,
    near_ss,
    near_rs,
    far_ss,
    far_rs,
    twin_ss,
    twin_rs,
    share_ss,
    share_rs,
    tiny_ss,
    tiny_rs,
    halo_ss,
    halo_rs,
    own_ss,
    own_rs,
    copy_sem,
):
    slots, segs, row_devs, local_rows, cols, chans, dps = geo
    per = slots // segs
    half = segs // MICRO
    ring = min(4, row_devs)
    lines = row_devs // ring
    far = half * lines
    plane = dps * row_devs
    piece = chans // plane
    part = chans // dps
    pos = local_rows * cols
    groups = chans // LANES
    wide = cols + 2 * DMAX
    chunks = cols // SUB
    population = IMG * local_rows * row_devs * cols
    seg = lax.axis_index("segment")
    row = lax.axis_index("rows")
    micro = seg // half
    core = lax.axis_index("dp")
    line = row // ring
    place = row % ring
    up = (row + row_devs - 1) % row_devs
    down = (row + 1) % row_devs
    has_up = row > 0
    has_down = row < row_devs - 1

    def near_peer(k):
        return {"rows": line * ring + (place + k) % ring}

    def far_peer(k):
        other = ((seg % half) * lines + line + k) % far
        return {"segment": micro * half + other // lines, "rows": other % lines * ring + place}

    def plane_index(k):
        return (core * row_devs + row + k) % plane

    def plane_peer(k):
        other = plane_index(k)
        return {"dp": other // row_devs, "rows": other % row_devs}

    def greet(k, carry):
        pl.semaphore_signal(barrier, inc=1, device_id=plane_peer(k), device_id_type=MESH)
        return carry

    def own_weight(b):
        return pltpu.make_async_copy(w_hbm.at[b], wv.at[seg * per + b], w_sem.at[b])

    inputs = (
        pltpu.make_async_copy(x_hbm.at[seg], xs.at[0, 1], in_sem.at[0]),
        pltpu.make_async_copy(cot_hbm.at[seg], cot_ref, in_sem.at[1]),
    )
    for copy in inputs:
        copy.start()
    for b in range(per):
        own_weight(b).start()

    barrier = pltpu.get_barrier_semaphore()
    lax.fori_loop(1, plane, greet, 0)
    for k in range(1, segs):
        pl.semaphore_signal(
            barrier, inc=1, device_id={"segment": (seg + k) % segs}, device_id_type=MESH)
    for k in range(1, far):
        if k % lines:
            other = (((seg % half) * lines + line + k) % far) // lines

            @pl.when(other != seg % half)
            def _():
                pl.semaphore_signal(barrier, inc=1, device_id=far_peer(k), device_id_type=MESH)
    pl.semaphore_wait(barrier, plane - 1 + segs - 1 + (half - 1) * (lines - 1))

    def halo_sends(step, src, up_dst, down_dst):
        a = pltpu.make_async_remote_copy(
            src, up_dst, halo_ss.at[step, 0], halo_rs.at[step, 0],
            device_id={"rows": up}, device_id_type=MESH)
        b = pltpu.make_async_remote_copy(
            src, down_dst, halo_ss.at[step, 1], halo_rs.at[step, 1],
            device_id={"rows": down}, device_id_type=MESH)
        return a, b

    def cot_sends():
        return halo_sends(2 * slots, cot_ref, coth.at[1], coth.at[0])

    def fwd_sends(j):
        return halo_sends(j, xs.at[j, 1], xs.at[j, 2], xs.at[j, 0])

    def bwd_sends(j):
        return halo_sends(slots + j, gpn.at[j], gph.at[j, 1], gph.at[j, 0])

    def near_send(step, k):
        return pltpu.make_async_remote_copy(
            stat_own.at[step], near_in.at[step, k - 1], near_ss.at[step], near_rs.at[step],
            device_id=near_peer(k), device_id_type=MESH)

    def far_send(step, k):
        return pltpu.make_async_remote_copy(
            stat_mid.at[step], far_in.at[step, k - 1], far_ss.at[step], far_rs.at[step],
            device_id=far_peer(k), device_id_type=MESH)

    def near_all(step):
        return pltpu.make_async_remote_copy(
            near_in.at[step], near_in.at[step], near_ss.at[step], near_rs.at[step],
            device_id=near_peer(1), device_id_type=MESH)

    def far_all(step):
        return pltpu.make_async_remote_copy(
            far_in.at[step], far_in.at[step], far_ss.at[step], far_rs.at[step],
            device_id=far_peer(1), device_id_type=MESH)

    def push_stats(step):
        for k in range(1, ring):
            near_send(step, k).start()

    def total_stats(step, meanwhile=None):
        near_all(step).wait_recv()
        mid = stat_own[step]
        for k in range(ring - 1):
            mid = mid + near_in[step, k]
        stat_mid[step] = mid
        for k in range(1, far):
            far_send(step, k).start()
        if meanwhile is not None:
            meanwhile()
        far_all(step).wait_recv()
        for k in range(far - 1):
            mid = mid + far_in[step, k]
        return mid

    def sent_stats(step):
        near_all(step).wait_send()
        far_all(step).wait_send()

    def to_owner(src, dst, slot, kind, owner):
        return pltpu.make_async_remote_copy(
            src, dst, own_ss.at[slot, kind], own_rs.at[slot % per, kind],
            device_id={"segment": owner}, device_id_type=MESH)

    def give(src, dst, slot, kind, owner):
        @pl.when(seg != owner)
        def _():
            to_owner(src, dst, slot, kind, owner).start()

        @pl.when(seg == owner)
        def _():
            pltpu.make_async_copy(src, dst, copy_sem.at[slot, kind]).start()

    def given(src, dst, slot, kind, owner):
        @pl.when(seg != owner)
        def _():
            to_owner(src, dst, slot, kind, owner).wait_send()

        @pl.when(seg == owner)
        def _():
            pltpu.make_async_copy(src, dst, copy_sem.at[slot, kind]).wait()

    def hid_args(j):
        return hs.at[j], hid_in.at[j % per, (seg - j // per + segs) % segs], j, 0, j // per

    def grad_args(j):
        return gs.at[j], grad_in.at[j % per, (seg - j // per + segs) % segs], j, 1, j // per

    def small_args(j):
        return small.at[j], small_in.at[j % per, (seg - j // per + segs) % segs], j, 2, j // per

    def sec_args(j):
        return xs.at[j + 1, 1], sec_in.at[seg], j, 3, j // per

    early = slots // 2
    mine = core * row_devs + row
    base = core * row_devs
    mate = {"dp": 1 - core}

    def away(j):
        return (seg - j // per + segs) % segs

    def remote(src, dst, ss, rs, j, where):
        return pltpu.make_async_remote_copy(
            src, dst, ss.at[j], rs.at[j], device_id=where, device_id_type=MESH)

    def moved(ss, rs, j, count):
        part_ref = wv.at[j, pl.ds(0, count)]
        return remote(part_ref, part_ref, ss, rs, j, mate)

    def half_ref(j):
        return wv.at[j, pl.ds(base, row_devs)]

    def place_peer(k):
        return {"rows": line * ring + (place + k) % ring}

    def line_peer(k):
        return {"rows": (line + k) % lines * ring + place}

    def first_count(j):
        return (ring if j % 2 == 0 else lines) - 1

    def second_count(j):
        return row_devs - 1 - first_count(j)

    def par_copy(k):
        return remote(
            pack_ref, par_ref.at[pl.ds(seg * per, per)], par_ss, par_rs, k - 1,
            {"segment": (seg + k) % segs})

    def seed(j):
        @pl.when(away(j) == 0)
        def _():
            if j < early:
                for k in range(1, segs):
                    remote(w_hbm.at[j % per, mine], wv.at[j, mine], x_ss, x_rs, j,
                           {"segment": (seg + k) % segs}).start()
            else:
                for k in (1, segs - 1):
                    remote(w_hbm.at[j % per, pl.ds(base, row_devs)], half_ref(j), two_ss, two_rs, j,
                           {"segment": (seg + k) % segs}).start()

    def phase_one(j):
        @pl.when(away(j) != 0)
        def _():
            moved(x_ss, x_rs, j, 1).wait_recv()
            for k in range(1, first_count(j) + 1):
                where = place_peer(k) if j % 2 == 0 else line_peer(k)
                remote(wv.at[j, mine], wv.at[j, mine], one_ss, one_rs, j, where).start()

    def phase_two(j):
        @pl.when(away(j) != 0)
        def _():
            if first_count(j):
                moved(one_ss, one_rs, j, first_count(j)).wait_recv()
            if j % 2 == 0:
                run = wv.at[j, pl.ds(base + line * ring, ring)]
                for k in range(1, lines):
                    remote(run, run, two_ss, two_rs, j, line_peer(k)).start()
            else:
                for k in range(1, ring):
                    for n in range(lines):
                        run = wv.at[j, base + n * ring + place]
                        remote(run, run, two_ss, two_rs, j, place_peer(k)).start()

    def to_mate(j):
        remote(half_ref(j), half_ref(j), mate_ss, mate_rs, j, mate).start()

    def relay(j):
        cut = row_devs // 2
        for near_seg, start, step in ((1, 0, 1), (segs - 1, cut, segs - 1)):
            @pl.when(away(j) == near_seg)
            def _():
                moved(two_ss, two_rs, j, row_devs).wait_recv()
                run = wv.at[j, pl.ds(base + start, cut)]
                remote(run, run, two_ss, two_rs, j, {"segment": (seg + step) % segs}).start()
                to_mate(j)

    def complete(j):
        if j < early:
            @pl.when(away(j) != 0)
            def _():
                if second_count(j):
                    moved(two_ss, two_rs, j, second_count(j)).wait_recv()
                to_mate(j)
        else:
            @pl.when(away(j) == 2)
            def _():
                moved(two_ss, two_rs, j, row_devs).wait_recv()
                to_mate(j)

    def sent_weights(j):
        @pl.when(away(j) == 0)
        def _():
            if j < early:
                moved(x_ss, x_rs, j, segs - 1).wait_send()
            else:
                moved(two_ss, two_rs, j, 2 * row_devs).wait_send()

        @pl.when(away(j) != 0)
        def _():
            moved(mate_ss, mate_rs, j, row_devs).wait_send()
            if j < early:
                if first_count(j):
                    moved(one_ss, one_rs, j, first_count(j)).wait_send()
                if second_count(j):
                    moved(two_ss, two_rs, j, second_count(j)).wait_send()

        if j >= early:
            for near_seg in (1, segs - 1):
                @pl.when(away(j) == near_seg)
                def _():
                    moved(two_ss, two_rs, j, row_devs // 2).wait_send()

    def during(j):
        for c in range(2, early):
            @pl.when(j == c - 2)
            def _():
                phase_two(c)
        for c in range(early, slots):
            @pl.when(j == c - 3)
            def _():
                relay(c)

        @pl.when(j == slots - 1)
        def _():
            for a in cot_sends():
                a.start()

    def after(j):
        for c in range(1, slots):
            @pl.when(j == c - 1)
            def _():
                complete(c)

    for k in range(1, segs):
        par_copy(k).start()
    for c in range(slots):
        seed(c)
    par_ref[pl.ds(seg * per, per)] = pack_ref[...]
    for c in range(early):
        phase_one(c)
    for c in range(2):
        phase_two(c)
    for copy in inputs:
        copy.wait()

    edge = jnp.zeros((DMAX * SUB, LANES), F32)

    def clear(j, carry):
        for r in range(3 * local_rows):
            apos[j, pl.ds(r * wide * SUB, DMAX * SUB), :] = edge
            apos[j, pl.ds((r * wide + DMAX + cols) * SUB, DMAX * SUB), :] = edge
        return carry

    lax.fori_loop(0, slots, clear, 0)
    for r in range(3 * local_rows):
        ghpos[pl.ds(r * wide * SUB, DMAX * SUB), :] = edge
        ghpos[pl.ds((r * wide + DMAX + cols) * SUB, DMAX * SUB), :] = edge

    def param(j, t):
        return par_ref[j, pl.ds(t * SUB, SUB), :]

    def tiles(value):
        return value.reshape(value.shape[0] // SUB, SUB, LANES)

    def flat(value):
        return value.reshape(-1, LANES)

    def spread_out(src, dst, base):
        for g in range(groups):
            dst[pl.ds(base * SUB + g, pos, stride=SUB), :] = src[:, g * LANES : (g + 1) * LANES].astype(F32)

    def own_rows(chunk):
        return chunk // chunks, chunk % chunks

    def at(p):
        return pl.ds(pl.multiple_of(p * SUB, SUB), SUB * SUB)

    def row_ok(value, r):
        if r < local_rows:
            return jnp.where(has_up, value, 0.0)
        if r >= 2 * local_rows:
            return jnp.where(has_down, value, 0.0)
        return value

    zero = jnp.zeros((SUB, LANES), F32)

    def reach(ref, lead, r, c, two):
        found = []
        for a in (-1, 0, 1):
            for b in (-1, 0, 1):
                both = [
                    tiles(ref[lead + (at((r + a * d) * wide + DMAX + c * SUB + b * d), slice(None))])
                    for d in ((1, 2) if a or b else (1,))
                ]
                found.append(jnp.where(two, both[1], both[0]) if len(both) > 1 else both[0])
        return found

    def switch(j, t):
        return jnp.broadcast_to(param(j, t), (SUB, SUB, LANES)) > 0.5

    def row_switch(j):
        return jnp.broadcast_to(par_ref[j, 11 * SUB : 11 * SUB + 1, :], (pos, LANES)) > 0.5

    def forward(j, carry):
        spread_out(xs.at[j, 1], xpos.at[j], pos)

        def sums(chunk, acc):
            v = tiles(xpos[j, at(pos + chunk * SUB), :])
            return acc[0] + jnp.sum(v, axis=0), acc[1] + jnp.sum(v * v, axis=0)

        s1, s2 = lax.fori_loop(0, pos // SUB, sums, (zero, zero))
        stat_own[j, 0:SUB, :] = s1
        stat_own[j, SUB : 2 * SUB, :] = s2
        push_stats(j)
        for a in fwd_sends(j):
            a.start()
        total = total_stats(j, lambda: during(j))

        @pl.when((j % per == 0) & (away(j) != 0))
        def _():
            first = pl.ds(j, per)
            pltpu.make_async_remote_copy(
                par_ref.at[first], par_ref.at[first], par_ss.at[0], par_rs.at[away(j) - 1],
                device_id=mate, device_id_type=MESH).wait_recv()

        center = total[0:SUB] / population
        spread = total[SUB : 2 * SUB] / population - center * center
        scaling = lax.rsqrt(spread + EPSILON)
        norms[j, 0:SUB, :] = center
        norms[j, SUB : 2 * SUB, :] = scaling
        gain = param(j, 9)
        shift = param(j, 10)

        def activate(r):
            def body(chunk, carry):
                v = tiles(xpos[j, at(r * cols + chunk * SUB), :])
                v = jnp.maximum((v - center) * scaling * gain + shift, 0.0)
                v = row_ok(v, r).astype(BF16).astype(F32)
                apos[j, at(r * wide + DMAX + chunk * SUB), :] = flat(v)
                return carry
            lax.fori_loop(0, chunks, body, 0)

        for r in range(local_rows, 2 * local_rows):
            activate(r)
        for side in range(2):
            fwd_sends(j)[side].wait_recv()
        spread_out(xs.at[j, 0], xpos.at[j], 0)
        spread_out(xs.at[j, 2], xpos.at[j], 2 * pos)
        for r in range(local_rows):
            activate(r)
            activate(2 * local_rows + r)
        two = switch(j, 12)
        taps = [param(j, t) for t in range(9)]

        def mix(chunk, carry):
            r, c = own_rows(chunk)
            acc = jnp.zeros((SUB, SUB, LANES), F32)
            for v, tap in zip(reach(apos, (j,), local_rows + r, c, two), taps):
                acc = acc + v * tap
            hpos[at(chunk * SUB), :] = flat(acc)
            return carry

        lax.fori_loop(0, pos // SUB, mix, 0)
        for g in range(groups):
            hs[j, :, g * LANES : (g + 1) * LANES] = hpos[pl.ds(g, pos, stride=SUB), :].astype(BF16)
        give(*hid_args(j))

        @pl.when(j == 0)
        def _():
            complete(0)

        @pl.when(away(j) == 0)
        def _():
            own_weight(j % per).wait()

        @pl.when(away(j) != 0)
        def _():
            moved(mate_ss, mate_rs, j, row_devs).wait_recv()

        step = chans // 4
        active = row_switch(j)
        for n in range(4):
            mixed = jnp.dot(
                hs[j], wv[j, :, :, n * step : (n + 1) * step].reshape(chans, step),
                preferred_element_type=F32)
            for k in range(step // LANES):
                cut = slice(n * step + k * LANES, n * step + (k + 1) * LANES)
                old = xs[j, 1, :, cut].astype(F32)
                new = old + mixed[:, k * LANES : (k + 1) * LANES]
                xs[j + 1, 1, :, cut] = jnp.where(active, new, old).astype(BF16)
        after(j)

        @pl.when(j % per == per - 1)
        def _():
            give(*sec_args(j))

        return carry

    lax.fori_loop(0, slots, forward, 0)

    for a in cot_sends():
        a.wait_recv()
    for side, src in enumerate((coth.at[0], cot_ref, coth.at[1])):
        for g in range(groups):
            v = src[:, g * LANES : (g + 1) * LANES].astype(F32)
            v = row_ok(v, side * local_rows)
            gpos[pl.ds(side * pos * SUB + g, pos, stride=SUB), :] = v
            gnat[side * pos : (side + 1) * pos, g * LANES : (g + 1) * LANES] = v.astype(BF16)

    def backward(t, carry):
        j = slots - 1 - t
        step = slots + j
        active = switch(j, 11)
        live = param(j, 11) > 0.5
        use = row_switch(j)
        for g in range(groups):
            cut = slice(g * LANES, (g + 1) * LANES)
            gs[j, :, cut] = jnp.where(use, gnat[pos : 2 * pos, cut].astype(F32), 0.0).astype(BF16)
        give(*grad_args(j))
        width = chans // 4
        for n in range(4):
            gh = lax.dot_general(
                gnat[...], wv[j].reshape(chans, chans)[n * width : (n + 1) * width],
                (((1,), (1,)), ((), ())), preferred_element_type=F32)
            gh = gh.astype(BF16).astype(F32)
            for k in range(width // LANES):
                g = n * (width // LANES) + k
                for r in range(3 * local_rows):
                    ghpos[pl.ds((r * wide + DMAX) * SUB + g, cols, stride=SUB), :] = gh[
                        r * cols : (r + 1) * cols, k * LANES : (k + 1) * LANES]
        two = switch(j, 12)
        taps = [param(j, k) for k in range(9)]
        gain = param(j, 9)
        shift = param(j, 10)
        center = norms[j, 0:SUB, :]
        scaling = norms[j, SUB : 2 * SUB, :]

        def pull(chunk, acc):
            r, c = own_rows(chunk)
            total = jnp.zeros((SUB, SUB, LANES), F32)
            for v, tap in zip(reach(ghpos, (), local_rows + r, c, two), taps[::-1]):
                total = total + v * tap
            normed = (tiles(xpos[j, at(pos + chunk * SUB), :]) - center) * scaling
            total = jnp.where(normed * gain + shift > 0, total, 0.0)
            gppos[at(pos + chunk * SUB), :] = flat(total)
            return acc[0] + jnp.sum(total, axis=0), acc[1] + jnp.sum(total * normed, axis=0)

        sum_a, sum_b = lax.fori_loop(0, pos // SUB, pull, (zero, zero))
        stat_own[step, 0:SUB, :] = sum_a
        stat_own[step, SUB : 2 * SUB, :] = sum_b

        @pl.when(j > 0)
        def _():
            push_stats(step)
            for g in range(groups):
                gpn[j, :, g * LANES : (g + 1) * LANES] = gppos[
                    pl.ds(pos * SUB + g, pos, stride=SUB), :].astype(BF16)
            for a in bwd_sends(j):
                a.start()

        def tap_grads(chunk, acc):
            r, c = own_rows(chunk)
            gh = tiles(ghpos[at((local_rows + r) * wide + DMAX + c * SUB), :])
            found = reach(apos, (j,), local_rows + r, c, two)
            return tuple(t + jnp.sum(v * gh, axis=0) for t, v in zip(acc, found))

        terms = lax.fori_loop(0, pos // SUB, tap_grads, (zero,) * 9)
        for k, term in enumerate(terms + (sum_b, sum_a)):
            small[j, k * SUB : (k + 1) * SUB, :] = jnp.where(live, term, 0.0)
        give(*small_args(j))

        @pl.when(j > 0)
        def _():
            total = total_stats(step)
            mean_a = total[0:SUB] / population
            mean_b = total[SUB : 2 * SUB] / population
            for side in range(2):
                bwd_sends(j)[side].wait_recv()
            spread_out(gph.at[j, 0], gppos, 0)
            spread_out(gph.at[j, 1], gppos, 2 * pos)
            factor = scaling * gain
            for r in range(3 * local_rows):
                def body(chunk, carry):
                    where = at(r * cols + chunk * SUB)
                    normed = (tiles(xpos[j, where, :]) - center) * scaling
                    old = tiles(gpos[where, :])
                    new = old + factor * (tiles(gppos[where, :]) - mean_a - normed * mean_b)
                    new = row_ok(jnp.where(active, new, old), r).astype(BF16).astype(F32)
                    gpos[where, :] = flat(new)
                    return carry
                lax.fori_loop(0, chunks, body, 0)
            for g in range(groups):
                gnat[:, g * LANES : (g + 1) * LANES] = gpos[pl.ds(g, 3 * pos, stride=SUB), :].astype(BF16)

        return carry

    lax.fori_loop(0, slots, backward, 0)

    def finish(j, carry):
        given(*hid_args(j))
        given(*grad_args(j))
        given(*small_args(j))
        for a in fwd_sends(j):
            a.wait_send()
        sent_stats(j)

        @pl.when(j % per == per - 1)
        def _():
            given(*sec_args(j))

        @pl.when(j > 0)
        def _():
            for a in bwd_sends(j):
                a.wait_send()
            sent_stats(slots + j)

        return carry

    lax.fori_loop(0, slots, finish, 0)
    for a in cot_sends():
        a.wait_send()
    for c in range(slots):
        sent_weights(c)
    for k in range(1, segs):
        par_copy(k).wait_send()

    def landed(dst, slot, kind):
        to_owner(dst, dst, slot, kind, (seg + 1) % segs).wait_recv()

    for k in range(per):
        landed(hid_in.at[k, pl.ds(1, segs - 1)], k, 0)
        landed(grad_in.at[k, pl.ds(1, segs - 1)], k, 1)
        landed(small_in.at[k, pl.ds(1, segs - 1)], k, 2)
    landed(sec_in.at[pl.ds(1, segs - 1)], per - 1, 3)
    sec_out[...] = sec_in[...]

    twin = {"dp": 1 - core}
    block = min(LANES, part)

    def outer(b, first):
        lhs = hid_in[b, :, :, pl.ds(pl.multiple_of(first, block), block)].reshape(segs * pos, block)
        return lax.dot_general(
            lhs, grad_in[b].reshape(segs * pos, chans),
            (((0,), (0,)), ((), ())), preferred_element_type=F32)

    def twin_send(b):
        return pltpu.make_async_remote_copy(
            twin_out.at[b], twin_in.at[b], twin_ss.at[b], twin_rs.at[b],
            device_id=twin, device_id_type=MESH)

    def share_send(b, k):
        other = (row + k) % row_devs
        return pltpu.make_async_remote_copy(
            half_sum.at[b, pl.ds(pl.multiple_of(other * piece, piece), piece)],
            share_in.at[b, k - 1], share_ss.at[b], share_rs.at[b],
            device_id={"rows": other}, device_id_type=MESH)

    def share_all(b):
        return pltpu.make_async_remote_copy(
            share_in.at[b], share_in.at[b], share_ss.at[b], share_rs.at[b],
            device_id={"rows": (row + 1) % row_devs}, device_id_type=MESH)

    def tiny_send(k):
        band = plane_index(k) * groups // plane
        return pltpu.make_async_remote_copy(
            tiny.at[band], tiny_in.at[k - 1], tiny_ss, tiny_rs,
            device_id=plane_peer(k), device_id_type=MESH)

    def tiny_all():
        return pltpu.make_async_remote_copy(
            tiny_in, tiny_in, tiny_ss, tiny_rs, device_id=plane_peer(1), device_id_type=MESH)

    def theirs(b):
        def body(n, carry):
            rows = pl.ds(pl.multiple_of(n * block, block), block)
            twin_out[b, rows, :] = outer(b, (1 - core) * part + n * block).astype(BF16)
            return carry
        lax.fori_loop(0, part // block, body, 0)
        twin_send(b).start()

    def ours(b):
        twin_send(b).wait_recv()

        def body(n, carry):
            rows = pl.ds(pl.multiple_of(n * block, block), block)
            value = outer(b, core * part + n * block) + twin_in[b, rows, :].astype(F32)
            half_sum[b, rows, :] = value.astype(BF16)
            return carry
        lax.fori_loop(0, part // block, body, 0)

        def push(k, carry):
            share_send(b, k).start()
            return carry
        lax.fori_loop(1, row_devs, push, 0)

    for b in range(per):
        theirs(b)
    rows = per * 11
    for b in range(per):
        total = jnp.sum(small_in[b], axis=0)
        gppos[b * 11 * SUB : (b + 1) * 11 * SUB, :] = total
    for g in range(groups):
        tiny[g, 0:rows, :] = gppos[pl.ds(g, rows, stride=SUB), :].astype(BF16)
        tiny[g, rows:, :] = jnp.zeros((32 - rows, LANES), BF16)

    def push_tiny(k, carry):
        tiny_send(k).start()
        return carry

    lax.fori_loop(1, plane, push_tiny, 0)
    for b in range(per):
        ours(b)
    tiny_all().wait_recv()
    small_out[...] = jnp.sum(tiny_in[...].astype(F32), axis=0) + tiny[
        plane_index(0) * groups // plane].astype(F32)
    for b in range(per):
        share_all(b).wait_recv()
        own = half_sum[b, pl.ds(pl.multiple_of(row * piece, piece), piece), :].astype(F32)
        for k in range(row_devs - 1):
            own = own + share_in[b, k].astype(F32)
        weight_out[b] = own
    for b in range(per):
        twin_send(b).wait_send()
        share_all(b).wait_send()
    tiny_all().wait_send()


def run_window(geo, images, cotangents, weights, params):
    slots, segs, row_devs, local_rows, cols, chans, dps = geo
    per = slots // segs
    pos = local_rows * cols
    ring = min(4, row_devs)
    far = segs // MICRO * (row_devs // ring)
    plane = dps * row_devs
    piece = chans // plane
    part = chans // dps
    wide = cols + 2 * DMAX
    ext = 3 * local_rows * wide * SUB
    vm = pltpu.VMEM
    dma = pltpu.SemaphoreType.DMA
    vmem = pl.BlockSpec(memory_space=pltpu.VMEM)
    return pl.pallas_call(
        functools.partial(window_kernel, geo),
        out_shape=(
            jax.ShapeDtypeStruct((segs, pos, chans), BF16),
            jax.ShapeDtypeStruct((per, piece, chans), F32),
            jax.ShapeDtypeStruct((32, LANES), F32),
        ),
        in_specs=[pl.BlockSpec(memory_space=pl.ANY)] * 3 + [vmem],
        out_specs=(vmem,) * 3,
        scratch_shapes=[
            vm((slots, plane, piece, chans), BF16),
            vm((slots + 1, 3, pos, chans), BF16),
            vm((slots, 3 * pos * SUB, LANES), F32),
            vm((slots, ext, LANES), F32),
            vm((pos * SUB, LANES), F32),
            vm((ext, LANES), F32),
            vm((3 * pos * SUB, LANES), F32),
            vm((3 * pos * SUB, LANES), F32),
            vm((3 * pos, chans), BF16),
            vm((slots, pos, chans), BF16),
            vm((slots, pos, chans), BF16),
            vm((slots, pos, chans), BF16),
            vm((slots, 2, pos, chans), BF16),
            vm((2, pos, chans), BF16),
            vm((2 * slots, 2 * SUB, LANES), F32),
            vm((2 * slots, 2 * SUB, LANES), F32),
            vm((2 * slots, ring - 1, 2 * SUB, LANES), F32),
            vm((2 * slots, far - 1, 2 * SUB, LANES), F32),
            vm((slots, 2 * SUB, LANES), F32),
            vm((slots, 11 * SUB, LANES), F32),
            vm((segs, pos, chans), BF16),
            vm((per, segs, pos, chans), BF16),
            vm((per, segs, pos, chans), BF16),
            vm((per, segs, 11 * SUB, LANES), F32),
            vm((per, part, chans), BF16),
            vm((per, part, chans), BF16),
            vm((per, part, chans), BF16),
            vm((per, row_devs - 1, piece, chans), BF16),
            vm((chans // LANES, 32, LANES), BF16),
            vm((plane - 1, 32, LANES), BF16),
            vm((slots, 13 * SUB, LANES), F32),
            vm((pos, chans), BF16),
            dma((2,)),
            dma((segs - 1,)),
            dma((segs - 1,)),
            dma((slots,)),
            dma((slots,)),
            dma((slots,)),
            dma((slots,)),
            dma((slots,)),
            dma((slots,)),
            dma((slots,)),
            dma((slots,)),
            dma((per,)),
            dma((2 * slots,)),
            dma((2 * slots,)),
            dma((2 * slots,)),
            dma((2 * slots,)),
            dma((per,)),
            dma((per,)),
            dma((per,)),
            dma((per,)),
            dma,
            dma,
            dma((2 * slots + 1, 2)),
            dma((2 * slots + 1, 2)),
            dma((slots, 4)),
            dma((per, 4)),
            dma((slots, 4)),
        ],
        compiler_params=pltpu.CompilerParams(
            collective_id=0, has_side_effects=True, vmem_limit_bytes=64000 * 1024),
        name="window",
    )(images, cotangents, weights, params)


def local(images, cotangent, pointwise, depthwise, norm_gain, norm_shift, cell_counts, dilations):
    segs = lax.axis_size("segment")
    row_devs = lax.axis_size("rows")
    dps = lax.axis_size("dp")
    per, chans = pointwise.shape[0], pointwise.shape[2]
    count, local_rows, cols, _ = images.shape
    slots = per * segs
    pos = local_rows * cols
    geo = (slots, segs, row_devs, local_rows, cols, chans, dps)
    plane = dps * row_devs
    piece = chans // plane
    index = lax.axis_index("dp") * row_devs + lax.axis_index("rows")
    flags = (jnp.arange(per, dtype=jnp.int32) < cell_counts[0]).astype(F32)
    pack = jnp.concatenate(
        [depthwise, norm_gain[:, None], norm_shift[:, None],
         jnp.broadcast_to(flags[:, None, None], (per, 1, chans)),
         jnp.broadcast_to((dilations > 1).astype(F32)[:, None, None], (per, 1, chans))], axis=1)
    sec, grad_weight, small = run_window(
        geo, images.reshape(count, pos, chans), cotangent.reshape(count, pos, chans),
        pointwise.reshape(per, plane, piece, chans), pack.reshape(per, 13 * SUB, LANES))
    small = small[: per * 11].reshape(per, 11, LANES)
    grad_small = lax.dynamic_slice_in_dim(small, index * piece % LANES, min(piece, LANES), 2)
    return (
        sec.reshape(1, count, local_rows, cols, chans),
        grad_weight,
        grad_small[:, :9],
        grad_small[:, 9:],
    )


def solution(mesh):
    return jax.shard_map(
        local,
        mesh=mesh,
        in_specs=(
            P("dp", "rows", None, None),
            P("dp", "rows", None, None),
            P("segment", None, None),
            P("segment", None, None),
            P("segment", None),
            P("segment", None),
            P("segment"),
            P("segment"),
        ),
        out_specs=(
            P("segment", "dp", "rows", None, None),
            P("segment", ("dp", "rows"), None),
            P("segment", None, ("dp", "rows")),
            P("segment", None, ("dp", "rows")),
        ),
        check_vma=False,
    )
```
